256 devices in a mesh: col: 32 (over z, y), row: 8 (over x, core).
Axes of the slice: x: 4, y: 4, z: 8, core: 2. Of those that a mesh axis runs over, the one named last changes fastest.
Arguments:
- panel: float32 [2, 12288, 6144], P(None, 'row', 'col'), may hold values from -0.078125 to 0.078125
- prior: float32 [6144, 64], P('col'), may hold values from -6 to 6
- right_side: float32 [2, 12288, 64], P(None, 'row'), may hold values from -6 to 6
- coupling: float32 [12288, 12288], P('row', 'col'), may hold values from -0.0546875 to 0.0546875
- inverses: float32 [2, 12288, 12288], P(None, 'row', 'col'), as said below
Outputs:
- solved: float32 [2, 12288, 64], P(None, 'row')
The draws below stay inside these ranges and needn't reach their ends.
Inputs may be any that keep to these rules, and one draw needn't show every extreme that they name: `inverses`: each of the two blocks is zero above its diagonal, and its diagonal lies between 0.5 and 2.
All inputs are finite; a program needn't handle non-finite values.
Results may differ from the reference program's by a relative error of at most 0.00011.
Values sent between devices are 32-bit elements; how exact they have to be, the bound alone decides.
No kernel may reach another device: no remote copies, remote signals or barrier semaphores. Data moves between devices by JAX's collectives and lax.ppermute only.
A program may use at most 64 MiB of HBM per device.

```python
import math
import jax
import jax.numpy as jnp
from jax import lax

NB = 12288
R = 64
K = 6144


def draw_inverses(key, part):
    inner = jax.random.fold_in(key, 11)
    key_below, key_diag = jax.random.split(inner)
    rows = lax.broadcasted_iota(jnp.int32, (2, NB, NB), 1)
    cols = lax.broadcasted_iota(jnp.int32, (2, NB, NB), 2)
    below = jax.random.normal(key_below, (2, NB, NB), jnp.float32) / math.sqrt(NB)
    diag = jnp.exp(jax.random.uniform(key_diag, (2, NB, 1), jnp.float32, math.log(0.5), math.log(2.0)))
    return jnp.where(rows > cols, below, jnp.where(rows == cols, diag, 0.0))


def levels(rng, extent, cuts, low, high):
    level = 1.0
    for axis_at, blocks in cuts:
        steps = jax.random.uniform(jax.random.fold_in(jax.random.fold_in(rng, 6), axis_at), (blocks,), jnp.float32, low / len(cuts), high / len(cuts))
        level = level * jnp.repeat(jnp.exp(steps), extent[axis_at] // blocks).reshape((-1,) + (1,) * (len(extent) - 1 - axis_at))
    return level


def normal_values(own_key, dims, spread, limit, pieces=(), kind=jnp.bfloat16):
    values = spread * jax.random.normal(own_key, dims, jnp.float32)
    if pieces:
        values = values * levels(own_key, dims, pieces, -0.22, 0.18)
    return jnp.clip(values, -limit, limit).astype(kind)


def setup_inputs(seed: int = 0) -> dict:
    key_list = jax.random.split(jax.random.key(seed), 6)
    return {
        "panel": normal_values(key_list[0], (2, NB, K), K ** -0.5, 0.078125, ((1, 8), (2, 32)), jnp.float32),
        "prior": normal_values(key_list[1], (K, R), 1.0, 6.0, ((0, 32),), jnp.float32),
        "right_side": normal_values(key_list[2], (2, NB, R), 1.0, 6.0, ((1, 8),), jnp.float32),
        "coupling": normal_values(key_list[3], (NB, NB), NB ** -0.5, 0.0546875, ((0, 8), (1, 32)), jnp.float32),
        "inverses": draw_inverses(jax.random.fold_in(key_list[5], 71), 0),
    }


def reference(panel, prior, right_side, coupling, inverses):
    highest = lax.Precision.HIGHEST
    carried = jnp.einsum("bik,kr->bir", panel, prior, precision=highest)
    first = right_side[0] - carried[0]
    leading = jnp.dot(inverses[0], first, precision=highest)
    second = right_side[1] - (carried[1] + jnp.dot(coupling, leading, precision=highest))
    trailing = jnp.dot(inverses[1], second, precision=highest)
    return jnp.stack([leading, trailing])
```

```python
import jax
import jax.numpy as jnp
from jax import lax
from jax.experimental import pallas as pl
from jax.experimental.pallas import tpu as pltpu
from jax.sharding import Mesh, PartitionSpec as P

ROW = ("x", "c")
COL = ("z", "y")
ALL = ("z", "y", "x", "c")
SLOT = (24, 128)
VMEM = pl.BlockSpec(memory_space=pltpu.VMEM)
HBM = pl.BlockSpec(memory_space=pltpu.HBM)


def grant(mib):
    return pltpu.CompilerParams(vmem_limit_bytes=mib << 20)


def halves(value):
    high = value.astype(jnp.bfloat16)
    low = (value - high.astype(jnp.float32)).astype(jnp.bfloat16)
    return high, low


def product(left, right, contract):
    left_high, left_low = halves(left)
    right_high, right_low = halves(right)
    dims = (((1,), (contract,)), ((), ()))
    both = lax.dot_general(
        jnp.concatenate([left_high, left_low], 0), right_high, dims, preferred_element_type=jnp.float32
    )
    rest = lax.dot_general(left_high, right_low, dims, preferred_element_type=jnp.float32)
    return both[:64] + (both[64:] + rest)


def put_slots(out_ref, value, start, add_ref=None):
    for at in range(value.shape[1] // 128):
        tile = start // 128 + at
        y, t = tile // 3, tile % 3
        for z in range(8):
            part = value[8 * z : 8 * z + 8, 128 * at : 128 * at + 128]
            if add_ref is not None:
                part = part + add_ref[4 * z + y, 8 * t : 8 * t + 8, :]
            out_ref[4 * z + y, 8 * t : 8 * t + 8, :] = part


def chunks(source, buffer, sems):
    copies = [pltpu.make_async_copy(source(g), buffer.at[g], sems.at[g]) for g in range(3)]
    for copy in copies:
        copy.start()
    for g in range(3):
        copies[g].wait()
        yield g


def carry_kernel(b, prior_ref, panel_ref, out_ref, buffer, sems):
    for g in chunks(lambda g: panel_ref.at[b, :, pl.ds(512 * g, 512)], buffer, sems):
        put_slots(out_ref, product(prior_ref[...], buffer[g], 0), 512 * g)


def carried(prior_t, panel_t, b):
    return pl.pallas_call(
        lambda *refs: carry_kernel(b, *refs),
        out_shape=jax.ShapeDtypeStruct((32, *SLOT), jnp.float32),
        in_specs=[VMEM, HBM],
        out_specs=VMEM,
        scratch_shapes=[pltpu.VMEM((3, 192, 512), jnp.float32), pltpu.SemaphoreType.DMA((3,))],
        compiler_params=grant(62),
        name=f"carry{b}",
    )(prior_t, panel_t)


def joined(gathered_ref):
    return jnp.concatenate(
        [jnp.concatenate([gathered_ref[e, 8 * t : 8 * t + 8, :] for t in range(3)], 1) for e in range(8)], 0
    )


def factor_kernel(b, gathered_ref, matrix_ref, *refs):
    *add, out_ref, buffer, sems = refs
    for g in chunks(lambda g: matrix_ref.at[b, pl.ds(512 * g, 512), :], buffer, sems):
        put_slots(out_ref, product(joined(gathered_ref), buffer[g], 1), 512 * g, *add)


def factor(gathered, matrix, b, *add):
    return pl.pallas_call(
        lambda *refs: factor_kernel(b, *refs),
        out_shape=jax.ShapeDtypeStruct((32, *SLOT), jnp.float32),
        in_specs=[VMEM, HBM] + [VMEM] * len(add),
        out_specs=VMEM,
        scratch_shapes=[pltpu.VMEM((3, 512, 384), jnp.float32), pltpu.SemaphoreType.DMA((3,))],
        compiler_params=grant(62),
        name="factor",
    )(gathered, matrix, *add)


def total_kernel(copies, parts_ref, *refs):
    out_ref = refs[-1]
    for t in range(3):
        rows = slice(8 * t, 8 * t + 8)
        sums = [parts_ref[k, rows, :] for k in range(4)]
        for s in range(4, 32):
            sums[s % 4] = sums[s % 4] + parts_ref[s, rows, :]
        value = (sums[0] + sums[1]) + (sums[2] + sums[3])
        if len(refs) > 1:
            value = refs[0][rows, :] - value
        for k in range(copies):
            out_ref[k, rows, :] = value


def total(parts, copies, base=None):
    args = [parts] if base is None else [parts, base]
    return pl.pallas_call(
        lambda *refs: total_kernel(copies, *refs),
        out_shape=jax.ShapeDtypeStruct((copies, *SLOT), jnp.float32),
        in_specs=[VMEM] * len(args),
        out_specs=VMEM,
        compiler_params=grant(4),
        name="total",
    )(*args)


def finish_kernel(leading_ref, trailing_ref, out_ref):
    for b, ref in enumerate((leading_ref, trailing_ref)):
        for z in range(8):
            for y in range(4):
                for t in range(3):
                    out_ref[b, 8 * z : 8 * z + 8, 384 * y + 128 * t : 384 * y + 128 * t + 128] = ref[
                        4 * z + y, 8 * t : 8 * t + 8, :
                    ]


def finish(leading, trailing):
    return pl.pallas_call(
        finish_kernel,
        out_shape=jax.ShapeDtypeStruct((2, 64, 1536), jnp.float32),
        in_specs=[VMEM] * 2,
        out_specs=VMEM,
        compiler_params=grant(8),
        name="finish",
    )(leading, trailing)


def exchanged(parts, axes):
    return lax.all_to_all(parts, axes, split_axis=0, concat_axis=0, tiled=True)


def device(z, y, row):
    return (z * 4 + y) * 8 + row


TURN = [(device(z, y, row), device(row, y, z)) for z in range(8) for y in range(4) for row in range(8)]


def spread(piece):
    turned = lax.ppermute(piece, ALL, TURN)
    return exchanged(jnp.broadcast_to(turned, (8, *SLOT)), ROW)


def shards(panel, prior, right_side, coupling, inverses):
    panel_t = panel.transpose(0, 2, 1)
    prior_t = prior.T
    right_t = right_side.transpose(0, 2, 1)
    z, y = lax.axis_index("z"), lax.axis_index("y")
    own = lax.dynamic_slice(right_t, (0, 8 * z, 384 * y), (2, 8, 384))
    own = own.reshape(2, 8, 3, 128).transpose(0, 2, 1, 3).reshape(2, *SLOT)

    first = total(exchanged(carried(prior_t, panel_t, 0), COL), 1, own[0])
    later = carried(prior_t, panel_t, 1)
    leading_parts = factor(spread(first), inverses, 0)
    leading = total(exchanged(leading_parts, COL), 1)
    second_parts = factor(spread(leading), coupling[None], 0, later)
    second = total(exchanged(second_parts, COL), 1, own[1])
    leading_all = exchanged(jnp.broadcast_to(leading, (32, *SLOT)), COL)
    trailing_parts = factor(spread(second), inverses, 1)
    trailing = total(exchanged(trailing_parts, COL), 32)
    trailing_all = exchanged(trailing, COL)
    return finish(leading_all, trailing_all).transpose(0, 2, 1)


def solution(mesh):
    fine = Mesh(mesh.devices.reshape(8, 4, 4, 2), ALL)
    in_specs = (
        P(None, ROW, COL),
        P(COL, None),
        P(None, ROW, None),
        P(ROW, COL),
        P(None, ROW, COL),
    )
    return jax.shard_map(shards, mesh=fine, in_specs=in_specs, out_specs=P(None, ROW, None), check_vma=False)
```

```python
import jax
import jax.numpy as jnp
from jax import lax
from jax.experimental import pallas as pl
from jax.experimental.pallas import tpu as pltpu
from jax.sharding import Mesh, PartitionSpec as P

ROW = ("x", "c")
COL = ("z", "y")
ALL = ("z", "y", "x", "c")
SLOT = (24, 128)
VMEM = pl.BlockSpec(memory_space=pltpu.VMEM)
HBM = pl.BlockSpec(memory_space=pltpu.HBM)


def grant(mib):
    return pltpu.CompilerParams(vmem_limit_bytes=mib << 20)


def halves(value):
    high = value.astype(jnp.bfloat16)
    low = (value - high.astype(jnp.float32)).astype(jnp.bfloat16)
    return high, low


def product(left, right, contract):
    left_high, left_low = halves(left)
    right_high, right_low = halves(right)
    dims = (((1,), (contract,)), ((), ()))
    both = lax.dot_general(
        jnp.concatenate([left_high, left_low], 0), right_high, dims, preferred_element_type=jnp.float32
    )
    rest = lax.dot_general(left_high, right_low, dims, preferred_element_type=jnp.float32)
    return both[:64] + (both[64:] + rest)


def put_slots(out_ref, value, start, add_ref=None):
    for at in range(value.shape[1] // 128):
        tile = start // 128 + at
        y, t = tile // 3, tile % 3
        for z in range(8):
            part = value[8 * z : 8 * z + 8, 128 * at : 128 * at + 128]
            if add_ref is not None:
                part = add_ref[4 * z + y, 8 * t : 8 * t + 8, :] - part
            out_ref[4 * z + y, 8 * t : 8 * t + 8, :] = part


def chunks(source, buffer, sems):
    copies = [pltpu.make_async_copy(source(g), buffer.at[g], sems.at[g]) for g in range(3)]
    for copy in copies:
        copy.start()
    for g in range(3):
        copies[g].wait()
        yield g


def carry_kernel(b, first_ref, prior_ref, panel_ref, right_ref, out_ref, buffer, sems):
    for g in chunks(lambda g: panel_ref.at[b, :, pl.ds(512 * g, 512)], buffer, sems):
        put_slots(out_ref, -product(prior_ref[...], buffer[g], 0), 512 * g)

    @pl.when(first_ref[0] == 1)
    def _():
        for z in range(8):
            for y in range(4):
                for t in range(3):
                    rows = slice(8 * t, 8 * t + 8)
                    lanes = 384 * y + 128 * t
                    out_ref[4 * z + y, rows, :] += right_ref[b, 8 * z : 8 * z + 8, lanes : lanes + 128]


def carried(first, prior_t, panel_t, right_t, b):
    return pl.pallas_call(
        lambda *refs: carry_kernel(b, *refs),
        out_shape=jax.ShapeDtypeStruct((32, *SLOT), jnp.float32),
        in_specs=[pl.BlockSpec(memory_space=pltpu.SMEM), VMEM, HBM, VMEM],
        out_specs=VMEM,
        scratch_shapes=[pltpu.VMEM((3, 192, 512), jnp.float32), pltpu.SemaphoreType.DMA((3,))],
        compiler_params=grant(62),
        name=f"carry{b}",
    )(first, prior_t, panel_t, right_t)


def joined(gathered_ref):
    return jnp.concatenate(
        [jnp.concatenate([gathered_ref[e, 8 * t : 8 * t + 8, :] for t in range(3)], 1) for e in range(8)], 0
    )


def factor_kernel(b, gathered_ref, matrix_ref, *refs):
    *add, out_ref, buffer, sems = refs
    for g in chunks(lambda g: matrix_ref.at[b, pl.ds(512 * g, 512), :], buffer, sems):
        put_slots(out_ref, product(joined(gathered_ref), buffer[g], 1), 512 * g, *add)


def factor(gathered, matrix, b, *add):
    return pl.pallas_call(
        lambda *refs: factor_kernel(b, *refs),
        out_shape=jax.ShapeDtypeStruct((32, *SLOT), jnp.float32),
        in_specs=[VMEM, HBM] + [VMEM] * len(add),
        out_specs=VMEM,
        scratch_shapes=[pltpu.VMEM((3, 512, 384), jnp.float32), pltpu.SemaphoreType.DMA((3,))],
        compiler_params=grant(62),
        name="factor",
    )(gathered, matrix, *add)


def total_kernel(copies, parts_ref, *refs):
    *with_ref, out_ref = refs
    at = 24 * len(with_ref)
    for t in range(3):
        rows = slice(8 * t, 8 * t + 8)
        sums = [parts_ref[k, rows, :] for k in range(4)]
        for s in range(4, 32):
            sums[s % 4] = sums[s % 4] + parts_ref[s, rows, :]
        value = (sums[0] + sums[1]) + (sums[2] + sums[3])
        for k in range(copies):
            for ref in with_ref:
                out_ref[k, rows, :] = ref[rows, :]
            out_ref[k, at + 8 * t : at + 8 * t + 8, :] = value


def total(parts, copies, *beside):
    return pl.pallas_call(
        lambda *refs: total_kernel(copies, *refs),
        out_shape=jax.ShapeDtypeStruct((copies, 24 + 24 * len(beside), 128), jnp.float32),
        in_specs=[VMEM] * (1 + len(beside)),
        out_specs=VMEM,
        compiler_params=grant(4),
        name="total",
    )(parts, *beside)


def finish_kernel(gathered_ref, out_ref):
    for b in range(2):
        for z in range(8):
            for y in range(4):
                for t in range(3):
                    lanes = 384 * y + 128 * t
                    rows = 24 * b + 8 * t
                    out_ref[b, 8 * z : 8 * z + 8, lanes : lanes + 128] = gathered_ref[4 * z + y, rows : rows + 8, :]


def finish(gathered):
    return pl.pallas_call(
        finish_kernel,
        out_shape=jax.ShapeDtypeStruct((2, 64, 1536), jnp.float32),
        in_specs=[VMEM],
        out_specs=VMEM,
        compiler_params=grant(8),
        name="finish",
    )(gathered)


def exchanged(parts, axes):
    return lax.all_to_all(parts, axes, split_axis=0, concat_axis=0, tiled=True)


def device(z, y, row):
    return (z * 4 + y) * 8 + row


TURN = [(device(z, y, row), device(row, y, z)) for z in range(8) for y in range(4) for row in range(8)]


def dealt(parts):
    return exchanged(parts.reshape(8, 96, 128), ROW).reshape(32, *SLOT)


def shards(panel, prior, right_side, coupling, inverses):
    panel_t = panel.transpose(0, 2, 1)
    prior_t = prior.T
    right_t = right_side.transpose(0, 2, 1)
    column = lax.axis_index("z") * 4 + lax.axis_index("y")
    first_column = (column == 0).astype(jnp.int32).reshape(1)

    first_parts = carried(first_column, prior_t, panel_t, right_t, 0)
    later = carried(first_column, prior_t, panel_t, right_t, 1)
    first = exchanged(total(exchanged(dealt(first_parts), COL), 8), ROW)
    first, later = lax.optimization_barrier((first, later))
    leading_parts = factor(first, inverses, 0)
    leading = total(exchanged(dealt(leading_parts), COL), 8)
    second_parts = factor(exchanged(leading, ROW), coupling[None], 0, later)
    second_dealt, piece = lax.optimization_barrier((dealt(second_parts), leading[0]))
    arrived, piece = lax.optimization_barrier((exchanged(second_dealt, COL), lax.ppermute(piece, ALL, TURN)))
    second = exchanged(total(arrived, 8), ROW)
    trailing_parts = factor(second, inverses, 1)
    both = total(exchanged(trailing_parts, COL), 32, piece)
    return finish(exchanged(both, COL)).transpose(0, 2, 1)


def solution(mesh):
    fine = Mesh(mesh.devices.reshape(8, 4, 4, 2), ALL)
    in_specs = (
        P(None, ROW, COL),
        P(COL, None),
        P(None, ROW, None),
        P(ROW, COL),
        P(None, ROW, COL),
    )
    return jax.shard_map(shards, mesh=fine, in_specs=in_specs, out_specs=P(None, ROW, None), check_vma=False)
```

```python
import jax
import jax.numpy as jnp
from jax import lax
from jax.experimental import pallas as pl
from jax.experimental.pallas import tpu as pltpu
from jax.sharding import Mesh, PartitionSpec as P

ROW = ("x", "c")
COL = ("z", "y")
ALL = ("z", "y", "x", "c")
DEAL = ("y", "x", "c")
SLOT = (24, 128)
VMEM = pl.BlockSpec(memory_space=pltpu.VMEM)
SMEM = pl.BlockSpec(memory_space=pltpu.SMEM)
HBM = pl.BlockSpec(memory_space=pltpu.HBM)


def grant(mib):
    return pltpu.CompilerParams(vmem_limit_bytes=mib << 20)


def array(*shape, dtype=jnp.float32):
    return jax.ShapeDtypeStruct(shape, dtype)


def halves(value):
    high = value.astype(jnp.bfloat16)
    low = (value - high.astype(jnp.float32)).astype(jnp.bfloat16)
    return high, low


def product(left, right_high, right_low, contract):
    left_high, left_low = halves(left)
    dims = (((1,), (contract,)), ((), ()))
    both = lax.dot_general(
        jnp.concatenate([left_high, left_low], 0), right_high, dims, preferred_element_type=jnp.float32
    )
    rest = lax.dot_general(left_high, right_low, dims, preferred_element_type=jnp.float32)
    return both[:64] + (both[64:] + rest)


def dealt_slot(z, y):
    return 8 * y + z


def column_slot(z, y):
    return 4 * z + y


def put_slots(slot, out_ref, value, start, add_ref=None):
    for at in range(value.shape[1] // 128):
        tile = start // 128 + at
        y, rows = tile // 3, slice(tile % 3 * 8, tile % 3 * 8 + 8)
        for z in range(8):
            part = value[8 * z : 8 * z + 8, 128 * at : 128 * at + 128]
            if add_ref is not None:
                part = add_ref[slot(z, y), rows, :] - part
            out_ref[slot(z, y), rows, :] = part


def carry_kernel(b, place_ref, prior_ref, panel_ref, right_ref, out_ref, buffer, piece, sems):
    z, y = place_ref[0], place_ref[1]
    copies = [
        pltpu.make_async_copy(panel_ref.at[b, :, pl.ds(512 * g, 512)], buffer.at[g], sems.at[g]) for g in range(3)
    ]
    copies.append(
        pltpu.make_async_copy(
            right_ref.at[b, pl.ds(pl.multiple_of(8 * z, 8), 8), pl.ds(pl.multiple_of(384 * y, 128), 384)],
            piece,
            sems.at[3],
        )
    )
    for copy in copies:
        copy.start()
    for g in range(3):
        copies[g].wait()
        put_slots(dealt_slot, out_ref, -product(prior_ref[...], *halves(buffer[g]), 0), 512 * g)
    copies[3].wait()
    own = dealt_slot(z, y)
    for t in range(3):
        out_ref[pl.ds(own, 1), 8 * t : 8 * t + 8, :] += piece[:, 128 * t : 128 * t + 128][None]


def carried(place, prior_t, panel_t, right_t, b):
    return pl.pallas_call(
        lambda *refs: carry_kernel(b, *refs),
        out_shape=array(32, *SLOT),
        in_specs=[SMEM, VMEM, HBM, HBM],
        out_specs=VMEM,
        scratch_shapes=[
            pltpu.VMEM((3, 192, 512), jnp.float32),
            pltpu.VMEM((8, 384), jnp.float32),
            pltpu.SemaphoreType.DMA((4,)),
        ],
        compiler_params=grant(62),
        name=f"carry{b}",
    )(place, prior_t, panel_t, right_t)


def split_kernel(matrix_ref, high_ref, low_ref):
    for start in range(0, 1536, 128):
        rows = slice(start, start + 128)
        high_ref[rows, :], low_ref[rows, :] = halves(matrix_ref[rows, :])


def split(matrix):
    return pl.pallas_call(
        split_kernel,
        out_shape=[array(1536, 384, dtype=jnp.bfloat16)] * 2,
        in_specs=[VMEM],
        out_specs=[VMEM] * 2,
        compiler_params=grant(4),
        name="split",
    )(matrix)


def joined(gathered_ref):
    return jnp.concatenate(
        [jnp.concatenate([gathered_ref[e, 8 * t : 8 * t + 8, :] for t in range(3)], 1) for e in range(8)], 0
    )


def factor_kernel(slot, gathered_ref, high_ref, low_ref, *refs):
    *add, out_ref = refs
    vector = joined(gathered_ref)
    for start in range(0, 1536, 512):
        rows = slice(start, start + 512)
        put_slots(slot, out_ref, product(vector, high_ref[rows, :], low_ref[rows, :], 1), start, *add)


def factor(slot, gathered, matrix, *add):
    return pl.pallas_call(
        lambda *refs: factor_kernel(slot, *refs),
        out_shape=array(32, *SLOT),
        in_specs=[VMEM] * (3 + len(add)),
        out_specs=VMEM,
        compiler_params=grant(8),
        name="factor",
    )(gathered, *matrix, *add)


def sum_of(values):
    values = list(values)
    while len(values) > 1:
        values = [a + b for a, b in zip(values[::2], values[1::2])]
    return values[0]


def fold_kernel(parts_ref, out_ref):
    for a in range(8):
        out_ref[a] = sum_of(parts_ref[8 * y + a] for y in range(4))


def fold(parts):
    return pl.pallas_call(
        fold_kernel,
        out_shape=array(8, *SLOT),
        in_specs=[VMEM],
        out_specs=VMEM,
        compiler_params=grant(4),
        name="fold",
    )(parts)


def total_kernel(copies, parts_ref, *refs):
    *with_ref, out_ref = refs
    at = 24 * len(with_ref)
    for t in range(3):
        rows = slice(8 * t, 8 * t + 8)
        value = sum_of(parts_ref[s, rows, :] for s in range(parts_ref.shape[0]))
        for k in range(copies):
            for ref in with_ref:
                out_ref[k, rows, :] = ref[rows, :]
            out_ref[k, at + 8 * t : at + 8 * t + 8, :] = value


def total(parts, copies, *beside):
    return pl.pallas_call(
        lambda *refs: total_kernel(copies, *refs),
        out_shape=array(copies, 24 + 24 * len(beside), 128),
        in_specs=[VMEM] * (1 + len(beside)),
        out_specs=VMEM,
        compiler_params=grant(4),
        name="total",
    )(parts, *beside)


def finish_kernel(gathered_ref, out_ref):
    for b in range(2):
        for z in range(8):
            for y in range(4):
                for t in range(3):
                    lanes = 384 * y + 128 * t
                    rows = 24 * b + 8 * t
                    out_ref[b, 8 * z : 8 * z + 8, lanes : lanes + 128] = gathered_ref[
                        column_slot(z, y), rows : rows + 8, :
                    ]


def finish(gathered):
    return pl.pallas_call(
        finish_kernel,
        out_shape=array(2, 64, 1536),
        in_specs=[VMEM],
        out_specs=VMEM,
        compiler_params=grant(8),
        name="finish",
    )(gathered)


def exchanged(parts, axes):
    return lax.all_to_all(parts, axes, split_axis=0, concat_axis=0, tiled=True)


def device(z, y, row):
    return (z * 4 + y) * 8 + row


TURN = [(device(z, y, row), device(row, y, z)) for z in range(8) for y in range(4) for row in range(8)]


def during(parts, axes, work, *operands):
    parts, operands = lax.optimization_barrier((parts, operands))
    return exchanged(parts, axes), work(*operands)


def shards(panel, prior, right_side, coupling, inverses):
    panel_t = panel.transpose(0, 2, 1)
    prior_t = prior.T
    right_t = right_side.transpose(0, 2, 1)
    place = jnp.stack([lax.axis_index("z"), lax.axis_index("y")]).astype(jnp.int32)

    def second_carry(panel_t):
        return carried(place, prior_t, panel_t, right_t, 1)

    first_parts = carried(place, prior_t, panel_t, right_t, 0)
    moved, later = during(first_parts, DEAL, second_carry, panel_t)
    moved = exchanged(fold(moved), "z")
    first, matrix = during(total(moved, 8), ROW, lambda m: split(m[0]), inverses)
    moved = exchanged(factor(dealt_slot, first, matrix), DEAL)
    leading = total(exchanged(fold(moved), "z"), 8)
    gathered, matrix = during(leading, ROW, split, coupling)
    second_parts = factor(dealt_slot, gathered, matrix, later)
    moved, piece = during(second_parts, DEAL, lambda p: lax.ppermute(p, ALL, TURN), leading[0])
    moved = exchanged(fold(moved), "z")
    second, matrix = during(total(moved, 8), ROW, lambda m: split(m[1]), inverses)
    trailing_parts = factor(column_slot, second, matrix)
    both = total(exchanged(trailing_parts, COL), 32, piece)
    return finish(exchanged(both, COL)).transpose(0, 2, 1)


def solution(mesh):
    fine = Mesh(mesh.devices.reshape(8, 4, 4, 2), ALL)
    in_specs = (
        P(None, ROW, COL),
        P(COL, None),
        P(None, ROW, None),
        P(ROW, COL),
        P(None, ROW, COL),
    )
    return jax.shard_map(shards, mesh=fine, in_specs=in_specs, out_specs=P(None, ROW, None), check_vma=False)
```

```python
import jax
import jax.numpy as jnp
from jax import lax
from jax.experimental import pallas as pl
from jax.experimental.pallas import tpu as pltpu
from jax.sharding import Mesh, PartitionSpec as P

ROW = ("x", "c")
COL = ("z", "y")
ALL = ("z", "y", "x", "c")
DEAL = ("y", "x", "c")
SLOT = (24, 128)
VMEM = pl.BlockSpec(memory_space=pltpu.VMEM)
SMEM = pl.BlockSpec(memory_space=pltpu.SMEM)
HBM = pl.BlockSpec(memory_space=pltpu.HBM)


def grant(mib):
    return pltpu.CompilerParams(vmem_limit_bytes=mib << 20)


def array(*shape, dtype=jnp.float32):
    return jax.ShapeDtypeStruct(shape, dtype)


def halves(value):
    high = value.astype(jnp.bfloat16)
    low = (value - high.astype(jnp.float32)).astype(jnp.bfloat16)
    return high, low


def product(left, right_high, right_low, contract):
    left_high, left_low = halves(left)
    dims = (((1,), (contract,)), ((), ()))
    both = lax.dot_general(
        jnp.concatenate([left_high, left_low], 0), right_high, dims, preferred_element_type=jnp.float32
    )
    rest = lax.dot_general(left_high, right_low, dims, preferred_element_type=jnp.float32)
    return both[:64] + (both[64:] + rest)


def dealt_slot(z, y):
    return 8 * y + z


def column_slot(z, y):
    return 4 * z + y


def put_slots(slot, out_ref, value, start, add_ref=None):
    for at in range(value.shape[1] // 128):
        tile = start // 128 + at
        y, rows = tile // 3, slice(tile % 3 * 8, tile % 3 * 8 + 8)
        for z in range(8):
            part = value[8 * z : 8 * z + 8, 128 * at : 128 * at + 128]
            if add_ref is not None:
                part = add_ref[slot(z, y), rows, :] - part
            out_ref[slot(z, y), rows, :] = part


def carry_kernel(b, prior_ref, panel_ref, right_ref, out_ref, prior, buffer, piece, slots, sems):
    z, y = lax.axis_index("z"), lax.axis_index("y")
    copies = [pltpu.make_async_copy(prior_ref, prior, sems.at[0])]
    for g in range(4):
        copies.append(pltpu.make_async_copy(panel_ref.at[b, :, pl.ds(384 * g, 384)], buffer.at[g], sems.at[1 + g]))
    copies.append(
        pltpu.make_async_copy(
            right_ref.at[b, pl.ds(pl.multiple_of(8 * z, 8), 8), pl.ds(pl.multiple_of(384 * y, 128), 384)],
            piece,
            sems.at[5],
        )
    )
    for copy in copies:
        copy.start()
    copies[0].wait()
    copies[5].wait()
    results = []
    for g in range(4):
        copies[1 + g].wait()
        put_slots(dealt_slot, slots, -product(prior[...], *halves(buffer[g]), 0), 384 * g)

        @pl.when(y == g)
        def _():
            for t in range(3):
                rows = slice(8 * t, 8 * t + 8)
                slots[pl.ds(8 * g + z, 1), rows, :] += piece[:, 128 * t : 128 * t + 128][None]

        results.append(pltpu.make_async_copy(slots.at[pl.ds(8 * g, 8)], out_ref.at[pl.ds(8 * g, 8)], sems.at[6 + g]))
        results[g].start()
    for result in results:
        result.wait()


def carried(prior_t, panel_t, right_t, b):
    return pl.pallas_call(
        lambda *refs: carry_kernel(b, *refs),
        out_shape=array(32, *SLOT),
        in_specs=[HBM] * 3,
        out_specs=HBM,
        scratch_shapes=[
            pltpu.VMEM((64, 192), jnp.float32),
            pltpu.VMEM((4, 192, 384), jnp.float32),
            pltpu.VMEM((8, 384), jnp.float32),
            pltpu.VMEM((32, *SLOT), jnp.float32),
            pltpu.SemaphoreType.DMA((10,)),
        ],
        compiler_params=grant(62),
        name=f"carry{b}",
    )(prior_t, panel_t, right_t)


def split_kernel(matrix_ref, high_ref, low_ref):
    for start in range(0, 1536, 128):
        rows = slice(start, start + 128)
        high_ref[rows, :], low_ref[rows, :] = halves(matrix_ref[rows, :])


def split(matrix):
    return pl.pallas_call(
        split_kernel,
        out_shape=[array(1536, 384, dtype=jnp.bfloat16)] * 2,
        in_specs=[VMEM],
        out_specs=[VMEM] * 2,
        compiler_params=grant(4),
        name="split",
    )(matrix)


def joined(gathered_ref):
    return jnp.concatenate(
        [jnp.concatenate([gathered_ref[e, 8 * t : 8 * t + 8, :] for t in range(3)], 1) for e in range(8)], 0
    )


def factor_kernel(slot, gathered_ref, high_ref, low_ref, *refs):
    *add, out_ref = refs
    vector = joined(gathered_ref)
    for start in range(0, 1536, 512):
        rows = slice(start, start + 512)
        put_slots(slot, out_ref, product(vector, high_ref[rows, :], low_ref[rows, :], 1), start, *add)


def factor(slot, gathered, matrix, *add):
    return pl.pallas_call(
        lambda *refs: factor_kernel(slot, *refs),
        out_shape=array(32, *SLOT),
        in_specs=[VMEM] * (3 + len(add)),
        out_specs=VMEM,
        compiler_params=grant(8),
        name="factor",
    )(gathered, *matrix, *add)


def sum_of(values):
    values = list(values)
    while len(values) > 1:
        values = [a + b for a, b in zip(values[::2], values[1::2])]
    return values[0]


def fold_kernel(parts_ref, out_ref):
    for a in range(8):
        out_ref[a] = sum_of(parts_ref[8 * y + a] for y in range(4))


def fold(parts):
    return pl.pallas_call(
        fold_kernel,
        out_shape=array(8, *SLOT),
        in_specs=[VMEM],
        out_specs=VMEM,
        compiler_params=grant(4),
        name="fold",
    )(parts)


def total_kernel(copies, parts_ref, out_ref):
    for t in range(3):
        rows = slice(8 * t, 8 * t + 8)
        value = sum_of(parts_ref[s, rows, :] for s in range(parts_ref.shape[0]))
        for k in range(copies):
            out_ref[k, rows, :] = value


def total(parts, copies):
    return pl.pallas_call(
        lambda *refs: total_kernel(copies, *refs),
        out_shape=array(copies, *SLOT),
        in_specs=[VMEM],
        out_specs=VMEM,
        compiler_params=grant(4),
        name="total",
    )(parts)


def lead_kernel(*refs):
    *quarter_refs, out_ref = refs
    y = lax.axis_index("y")
    for shift, ref in enumerate(quarter_refs):
        own = lax.rem(y + 4 - shift, 4)
        for z in range(8):
            for t in range(3):
                lanes = pl.ds(pl.multiple_of(384 * own + 128 * t, 128), 128)
                out_ref[0, 8 * z : 8 * z + 8, lanes] = ref[z, 8 * t : 8 * t + 8, :]


def lead(quarters):
    return pl.pallas_call(
        lead_kernel,
        out_shape=array(2, 64, 1536),
        grid=(1,),
        in_specs=[pl.BlockSpec((8, *SLOT), lambda g: (0, 0, 0))] * 4,
        out_specs=pl.BlockSpec((1, 64, 1536), lambda g: (0, 0, 0)),
        compiler_params=grant(8),
        name="lead",
    )(*quarters)


def finish_kernel(gathered_ref, _, out_ref):
    for z in range(8):
        for y in range(4):
            for t in range(3):
                lanes = 384 * y + 128 * t
                out_ref[0, 8 * z : 8 * z + 8, lanes : lanes + 128] = gathered_ref[
                    column_slot(z, y), 8 * t : 8 * t + 8, :
                ]


def finish(gathered, solved):
    return pl.pallas_call(
        finish_kernel,
        out_shape=array(2, 64, 1536),
        grid=(1,),
        in_specs=[pl.BlockSpec((32, *SLOT), lambda g: (0, 0, 0)), HBM],
        out_specs=pl.BlockSpec((1, 64, 1536), lambda g: (1, 0, 0)),
        input_output_aliases={1: 0},
        compiler_params=grant(8),
        name="finish",
    )(gathered, solved)


def exchanged(parts, axes):
    return lax.all_to_all(parts, axes, split_axis=0, concat_axis=0, tiled=True)


def device(z, y, row):
    return (z * 4 + y) * 8 + row


TURN = [(device(z, y, row), device(row, y, z)) for z in range(8) for y in range(4) for row in range(8)]


def turned(gathered):
    return lax.ppermute(gathered, ALL, TURN)


def quarters(own):
    return [own] + [lax.ppermute(own, "y", [(y, (y + shift) % 4) for y in range(4)]) for shift in range(1, 4)]


def during(parts, axes, work, *operands):
    parts, operands = lax.optimization_barrier((parts, operands))
    return exchanged(parts, axes), work(*operands)


def shards(panel, prior, right_side, coupling, inverses):
    panel_t = panel.transpose(0, 2, 1)
    prior_t = prior.T
    right_t = right_side.transpose(0, 2, 1)

    def second_carry(panel_t):
        return carried(prior_t, panel_t, right_t, 1)

    first_parts = carried(prior_t, panel_t, right_t, 0)
    moved, later = lax.optimization_barrier(during(first_parts, DEAL, second_carry, panel_t))
    moved = exchanged(fold(moved), "z")
    first, matrix = during(total(moved, 8), ROW, lambda m: split(m[0]), inverses)
    moved = exchanged(factor(dealt_slot, first, matrix), DEAL)
    leading = total(exchanged(fold(moved), "z"), 8)
    gathered, matrix = during(leading, ROW, split, coupling)
    second_parts = factor(dealt_slot, gathered, matrix, later)
    moved, quarter = during(second_parts, DEAL, turned, gathered)
    moved, quarter = lax.optimization_barrier((moved, quarter))
    moved = exchanged(fold(moved), "z")
    second, matrix = during(total(moved, 8), ROW, lambda m: split(m[1]), inverses)
    trailing_parts = factor(column_slot, second, matrix)
    moved, leading_quarters = during(trailing_parts, COL, quarters, quarter)
    moved, leading_quarters = lax.optimization_barrier((moved, leading_quarters))
    trailing, solved = during(total(moved, 32), COL, lambda *q: lead(q), *leading_quarters)
    return finish(trailing, solved).transpose(0, 2, 1)


def solution(mesh):
    fine = Mesh(mesh.devices.reshape(8, 4, 4, 2), ALL)
    in_specs = (
        P(None, ROW, COL),
        P(COL, None),
        P(None, ROW, None),
        P(ROW, COL),
        P(None, ROW, COL),
    )
    return jax.shard_map(shards, mesh=fine, in_specs=in_specs, out_specs=P(None, ROW, None), check_vma=False)
```
